32 devices in a mesh: sec: 4 (over y, x), strip: 8 (over z, core).
Axes of the slice: x: 2, y: 2, z: 4, core: 2. Of those that a mesh axis runs over, the one named last changes fastest.
Arguments:
- activations: bfloat16 [2, 4, 1, 2, 1, 256, 64, 512], P(None, 'sec', None, None, None, 'strip'), may hold values from 0 to 2
- relu_masks: int32 [2, 4, 1, 2, 1, 256, 64, 512], P(None, 'sec', None, None, None, 'strip'), may hold values 0 or 1
- grad_in: bfloat16 [2, 2, 1, 256, 64, 512], P(None, None, None, 'strip'), may hold values from -6 to 6
- mix_weight: bfloat16 [4, 1, 512, 512], P('sec'), may hold values from -0.375 to 0.375
- depth_kernel: bfloat16 [4, 1, 25, 512], P('sec'), may hold values from -1.25 to 1.25
Outputs:
- segment_grads: bfloat16 [2, 4, 2, 1, 256, 64, 512], P(None, 'sec', None, None, 'strip')
- mix_grad: float32 [4, 1, 512, 512], P('sec', None, 'strip')
- kernel_grad: float32 [4, 1, 25, 512], P('sec')
The draws below stay inside these ranges and needn't reach their ends.
All inputs are finite; a program needn't handle non-finite values. No bound on the sum of `relu_masks` on one device may be relied on, other than what follows from the above.
Results may differ from the reference program's by a relative error of at most 0.025.
Values may be sent and summed in bfloat16 or wider, within the bound.
A program may use at most 192 MiB of HBM per device.

```python
import jax
import jax.numpy as jnp
from jax import lax

C = 512
H = 256
W = 64
LAYERS = 1
MICRO = 2
IMAGES = 1
SECTIONS = 4


def plant(array, rng, least, largest):
    longest = array.shape.index(max(array.shape))
    spots = []
    for shift in (0, 1):
        where = [jax.random.randint(jax.random.fold_in(rng, axis), (), 0, length) for axis, length in enumerate(array.shape)]
        where[longest] = (where[longest] + shift) % array.shape[longest]
        spots.append(tuple(where))
    return array.at[spots[0]].set(least).at[spots[1]].set(largest)


def levels(rng, extent, cuts, smallest, high):
    loudness = 1.0
    for axis_at, blocks in cuts:
        heights = jax.random.uniform(jax.random.fold_in(jax.random.fold_in(rng, 6), axis_at), (blocks,), jnp.float32, smallest / len(cuts), high / len(cuts))
        loudness = loudness * jnp.repeat(jnp.exp(heights), extent[axis_at] // blocks).reshape((-1,) + (1,) * (len(extent) - 1 - axis_at))
    return loudness


def normal_values(key, extent, spread, bound, split=(), dtype=jnp.bfloat16):
    entries = spread * jax.random.normal(key, extent, jnp.float32)
    if split:
        entries = entries * levels(key, extent, split, -0.22, 0.18)
    return jnp.clip(entries, -bound, bound).astype(dtype)


def setup_inputs(seed: int = 0) -> dict:
    key_of = jax.random.split(jax.random.key(seed), 6)
    activations = jnp.clip(2.0 * jax.random.uniform(key_of[0], (2, SECTIONS, LAYERS, MICRO, IMAGES, H, W, C), jnp.float32) ** levels(key_of[0], (2, SECTIONS, LAYERS, MICRO, IMAGES, H, W, C), ((1, 4), (5, 8)), -0.2, 0.2), 0.0, 2.0).astype(jnp.bfloat16)
    relu_masks = plant((jax.random.randint(key_of[1], (2, SECTIONS, LAYERS, MICRO, IMAGES, H, W, C), 0, 2) < 1).astype(jnp.int32), jax.random.fold_in(key_of[1], 1), 0, 1)
    grad_in = normal_values(key_of[2], (2, MICRO, IMAGES, H, W, C), 1.0, 6.0, ((3, 8),))
    mix_weight = normal_values(key_of[3], (SECTIONS, LAYERS, C, C), (C // 2) ** -0.5, 0.375, ((0, 4),))
    depth_kernel = normal_values(key_of[4], (SECTIONS, LAYERS, 25, C), 25 ** -0.5, 1.25, ((0, 4),))
    return {"activations": activations, "relu_masks": relu_masks, "grad_in": grad_in, "mix_weight": mix_weight, "depth_kernel": depth_kernel}


def forward_depth(layer_input, kernel):
    framed = jnp.pad(layer_input.astype(jnp.float32), ((0, 0), (2, 2), (2, 2), (0, 0)))
    rows, cols = layer_input.shape[1], layer_input.shape[2]
    total = jnp.zeros(layer_input.shape, jnp.float32)
    for row_tap in range(5):
        for col_tap in range(5):
            window = framed[:, row_tap:row_tap + rows, col_tap:col_tap + cols, :]
            total = total + window * kernel[row_tap * 5 + col_tap].astype(jnp.float32)
    return total, framed


def transposed_depth(back_mix, kernel):
    framed = jnp.pad(back_mix.astype(jnp.float32), ((0, 0), (2, 2), (2, 2), (0, 0)))
    rows, cols = back_mix.shape[1], back_mix.shape[2]
    total = jnp.zeros(back_mix.shape, jnp.float32)
    for row_tap in range(5):
        for col_tap in range(5):
            window = framed[:, 4 - row_tap:4 - row_tap + rows, 4 - col_tap:4 - col_tap + cols, :]
            total = total + window * kernel[row_tap * 5 + col_tap].astype(jnp.float32)
    return total


def kernel_corr(back_mix, framed):
    rows, cols = back_mix.shape[1], back_mix.shape[2]
    wide = back_mix.astype(jnp.float32)
    terms = []
    for row_tap in range(5):
        for col_tap in range(5):
            window = framed[:, row_tap:row_tap + rows, col_tap:col_tap + cols, :]
            terms.append(jnp.sum(wide * window, axis=(0, 1, 2)))
    return jnp.stack(terms)


def section_back(upstream, layer_inputs, layer_masks, weight, kernel):
    channels = upstream.shape[-1]
    weight_terms = []
    kernel_terms = []
    for layer in reversed(range(layer_inputs.shape[0])):
        depth, framed = forward_depth(layer_inputs[layer], kernel[layer])
        depth = depth.astype(jnp.bfloat16)
        gated = jnp.where(layer_masks[layer] == 1, upstream, jnp.zeros_like(upstream))
        flat_gated = gated.reshape(-1, channels)
        back_mix = jnp.dot(flat_gated, weight[layer].T, preferred_element_type=jnp.float32)
        back_mix = back_mix.astype(jnp.bfloat16).reshape(upstream.shape)
        weight_terms.insert(0, jnp.dot(depth.reshape(-1, channels).T, flat_gated, preferred_element_type=jnp.float32))
        kernel_terms.insert(0, kernel_corr(back_mix, framed))
        upstream = transposed_depth(back_mix, kernel[layer]).astype(jnp.bfloat16)
    return upstream, jnp.stack(weight_terms), jnp.stack(kernel_terms)


def reference(activations, relu_masks, grad_in, mix_weight, depth_kernel):
    weight_sums = jnp.zeros(mix_weight.shape, jnp.float32)
    kernel_sums = jnp.zeros(depth_kernel.shape, jnp.float32)
    replicas = []
    for replica in range(2):
        if replica == 0:
            weights, kernels = mix_weight, depth_kernel
        else:
            weights, kernels = jnp.flip(mix_weight, 0), jnp.flip(depth_kernel, 0)
        per_micro = []
        for micro in range(MICRO):
            def segment(upstream, inputs):
                layer_inputs, layer_masks, weight, kernel = inputs
                result, weight_term, kernel_term = section_back(upstream, layer_inputs, layer_masks, weight, kernel)
                return result, (result, weight_term, kernel_term)

            carried, (results, weight_terms, kernel_terms) = lax.scan(
                segment, grad_in[replica, micro],
                (activations[replica, :, :, micro], relu_masks[replica, :, :, micro], weights, kernels),
                reverse=(replica == 0))
            if replica == 1:
                weight_terms = jnp.flip(weight_terms, 0)
                kernel_terms = jnp.flip(kernel_terms, 0)
            weight_sums = weight_sums + weight_terms
            kernel_sums = kernel_sums + kernel_terms
            per_micro.append(results)
        replicas.append(jnp.stack(per_micro, axis=1))
    return jnp.stack(replicas), weight_sums * (1.0 / H), kernel_sums * (1.0 / H)
```

```python
import functools

import jax
import jax.numpy as jnp
from jax import lax
from jax.experimental import pallas as pl
from jax.experimental.pallas import tpu as pltpu
from jax.sharding import PartitionSpec as P

H = 256
LANES = 128
PAIR = 2 * LANES
BF = jnp.bfloat16
ANY = pl.BlockSpec(memory_space=pl.ANY)
VMEM = pl.BlockSpec(memory_space=pltpu.VMEM)
MESH = pl.DeviceIdType.MESH


def lane_block(block):
    return pl.ds(pl.multiple_of(block * LANES, LANES), LANES)


def shifted(value, offset, column):
    if offset == 0:
        return value
    cols = value.shape[0]
    turned = pltpu.roll(value, (-offset) % cols, 0)
    inside = column < cols - offset if offset > 0 else column >= -offset
    return jnp.where(inside, turned, 0.0)


def spread_kernels(kern, conv_w):
    blocks = conv_w.shape[1]
    same = lax.broadcasted_iota(jnp.int32, (LANES, LANES), 0) == lax.broadcasted_iota(jnp.int32, (LANES, LANES), 1)

    @pl.loop(0, 2 * blocks)
    def _(i):
        r = i // blocks
        b = i % blocks
        lanes = lane_block(b)
        for j in range(5):
            for t in range(3):
                for e in range(2):
                    for f in range(2):
                        d = 2 * t + e - f
                        if 0 <= d < 5:
                            tap = jnp.broadcast_to(kern[r, pl.ds(5 * d + j, 1), lanes], (LANES, LANES))
                            tile = jnp.where(same, tap, 0.0).astype(BF)
                        else:
                            tile = jnp.zeros((LANES, LANES), BF)
                        conv_w[r, b, pl.ds((3 * j + t) * PAIR + e * LANES, LANES), f * LANES : (f + 1) * LANES] = tile


def section_kernel(
    sections, strips, micro, rows, cols, channels,
    acts, masks, entry, weight, kern,
    sg, wout, kout, saved,
    gated, seen, framed, act_halo, mixed, edge, halo, wide, out, conv_w, ksum,
    send, recv, halo_send, halo_recv, act_send, act_recv, loads, stores,
):
    p = lax.axis_index("sec")
    s = lax.axis_index("strip")
    blocks = channels // LANES
    pairs = rows // 2
    first = 1 - (2 * p) // sections
    column = lax.broadcasted_iota(jnp.int32, (cols, LANES), 0)

    barrier = pltpu.get_barrier_semaphore()
    near = [(p > 0, (p - 1, s)), (p < sections - 1, (p + 1, s)), (s > 0, (p, s - 1)), (s < strips - 1, (p, s + 1))]
    for there, device in near:
        @pl.when(there)
        def _(device=device):
            pl.semaphore_signal(barrier, inc=1, device_id=device, device_id_type=MESH)
    pl.semaphore_wait(barrier, sum(jnp.where(there, 1, 0) for there, _ in near))

    to_side = [s < strips - 1, s > 0]
    from_side = [s > 0, s < strips - 1]
    side_of = [(p, s + 1), (p, s - 1)]

    def act_copy(side):
        lines = pl.ds(rows - 2, 2) if side == 0 else pl.ds(0, 2)
        return pltpu.make_async_remote_copy(
            src_ref=acts.at[:, 0, 0, :, 0, lines], dst_ref=act_halo.at[side],
            send_sem=act_send.at[side], recv_sem=act_recv.at[side], device_id=side_of[side], device_id_type=MESH)

    def halo_copy(u, side):
        return pltpu.make_async_remote_copy(
            src_ref=edge.at[u, side], dst_ref=halo.at[u, side],
            send_sem=halo_send.at[u, side], recv_sem=halo_recv.at[u, side], device_id=side_of[side], device_id_type=MESH)

    def main_copy(r, m, b):
        u = r * micro + m
        lanes = lane_block(b)
        return pltpu.make_async_remote_copy(
            src_ref=out.at[m, :, :, lanes], dst_ref=gated.at[u, :, :, lanes],
            send_sem=send.at[u, b], recv_sem=recv.at[u, b], device_id=(p + 2 * r - 1, s), device_id_type=MESH)

    def has_next(r):
        return jnp.logical_or(jnp.logical_and(r == 0, p > 0), jnp.logical_and(r == 1, p < sections - 1))

    def out_store(r, m):
        return pltpu.make_async_copy(out.at[m], sg.at[r, m], stores.at[r * micro + m])

    def drain(r, m):
        @pl.when(has_next(r))
        def _():
            @pl.loop(0, blocks)
            def _(b):
                main_copy(r, m, b).wait_send()
        out_store(r, m).wait()

    for side in range(2):
        @pl.when(to_side[side])
        def _(side=side):
            act_copy(side).start()

        @pl.when(jnp.logical_not(from_side[side]))
        def _(side=side):
            act_halo[side] = jnp.zeros_like(act_halo[side])

    spread_kernels(kern, conv_w)
    ksum[...] = jnp.zeros_like(ksum)
    wout[...] = jnp.zeros_like(wout)
    for side in range(2):
        @pl.when(from_side[side])
        def _(side=side):
            act_copy(side).wait_recv()

    def widen(line_of, place, swap, count):
        @pl.loop(0, count * blocks)
        def _(i):
            g = i // blocks
            b = i % blocks
            for par in range(2):
                value = line_of(g, par, lane_block(b)).astype(jnp.float32)
                at = (1 - par if swap else par) * LANES
                for j in range(5):
                    wide[b, j, place + g, :, at : at + LANES] = shifted(value, j - 2, column).astype(BF)

    def load_acts(r, m):
        return pltpu.make_async_copy(acts.at[r, 0, 0, m, 0], framed.at[pl.ds(2, rows)], loads.at[0])

    def frame(r, m):
        framed[pl.ds(0, 2)] = act_halo[0, r, m]
        framed[pl.ds(rows + 2, 2)] = act_halo[1, r, m]

    def conv(r, b, flip):
        parts = []
        for j in range(5):
            for t in range(3):
                part = wide[b, 4 - j, pl.ds(2 - t, pairs)] if flip else wide[b, j, pl.ds(t, pairs)]
                parts.append(part.reshape(pairs * cols, PAIR))
        made = jnp.dot(jnp.concatenate(parts, axis=1), conv_w[r, b], preferred_element_type=jnp.float32)
        return made.astype(BF).reshape(pairs, cols, PAIR)

    def chain(r, m):
        u = r * micro + m
        load_mask = pltpu.make_async_copy(masks.at[r, 0, 0, m, 0], seen, loads.at[1])
        load_mask.start()
        load_acts(r, m).start()
        fresh = jnp.logical_not(has_next(1 - r))

        @pl.when(fresh)
        def _():
            load = pltpu.make_async_copy(entry.at[r, m, 0], gated.at[u], loads.at[2])
            load.start()
            load.wait()

        @pl.when(jnp.logical_not(fresh))
        def _():
            @pl.loop(0, blocks)
            def _(b):
                main_copy(r, m, b).wait_recv()

        load_mask.wait()

        @pl.loop(0, rows)
        def _(row):
            value = gated[u, row].astype(jnp.float32)
            gated[u, row] = jnp.where(seen[row] == 1, value, 0.0).astype(BF)

        ends = jnp.concatenate([gated[u, pl.ds(rows - 2, 2)], gated[u, pl.ds(0, 2)]], axis=0)
        made = lax.dot_general(ends.reshape(4 * cols, channels), weight[r], (((1,), (1,)), ((), ())),
                               preferred_element_type=jnp.float32)
        edge[u] = made.astype(BF).reshape(2, 2, cols, channels)
        for side in range(2):
            @pl.when(to_side[side])
            def _(side=side):
                halo_copy(u, side).start()

            @pl.when(jnp.logical_not(from_side[side]))
            def _(side=side):
                halo[u, side] = jnp.zeros_like(halo[u, side])

        @pl.loop(0, rows // 16)
        def _(i):
            lines = pl.ds(i * 16, 16)
            got = lax.dot_general(gated[u, lines].reshape(16 * cols, channels), weight[r], (((1,), (1,)), ((), ())),
                                  preferred_element_type=jnp.float32)
            mixed[lines] = got.astype(BF).reshape(16, cols, channels)

        widen(lambda g, par, lanes: mixed[2 * g + par, :, lanes], 1, True, pairs)
        for side in range(2):
            @pl.when(from_side[side])
            def _(side=side):
                halo_copy(u, side).wait_recv()
        widen(lambda g, par, lanes: halo[u, 0, par, :, lanes], 0, True, 1)
        widen(lambda g, par, lanes: halo[u, 1, par, :, lanes], pairs + 1, True, 1)

        @pl.when(r != first)
        def _():
            drain(first, m)

        @pl.loop(0, blocks)
        def _(b):
            made = conv(r, b, True)
            lanes = lane_block(b)
            for par in range(2):
                piece = made[:, :, (1 - par) * LANES : (2 - par) * LANES]
                for q in range(pairs):
                    out[m, 2 * q + par, :, lanes] = piece[q]

            @pl.when(has_next(r))
            def _():
                main_copy(r, m, b).start()

        out_store(r, m).start()
        load_acts(r, m).wait()
        frame(r, m)

        @pl.loop(0, blocks * 5)
        def _(i):
            b = i // 5
            j = i % 5
            lanes = lane_block(b)

            def rows_of(q, totals):
                near_rows = [framed[2 * q + k, :, lanes].reshape(cols // 16, 16, LANES) for k in range(6)]
                both = wide[b, 4 - j, q + 1]
                fresh_totals = []
                for d in range(5):
                    terms = []
                    for par in range(2):
                        line = both[:, (1 - par) * LANES : (2 - par) * LANES].reshape(cols // 16, 16, LANES)
                        part = line * near_rows[par + d]
                        terms += [part[k] for k in range(cols // 16)]
                    while len(terms) > 1:
                        terms = [terms[k] + terms[k + 1] for k in range(0, len(terms), 2)]
                    short = jnp.sum(terms[0].astype(jnp.float32).reshape(2, 8, LANES), axis=0)
                    fresh_totals.append(totals[d] + short)
                return tuple(fresh_totals)

            zero = jnp.zeros((8, LANES), jnp.float32)
            totals = lax.fori_loop(0, pairs, rows_of, (zero,) * 5)
            for d in range(5):
                ksum[r, 5 * d + j, :, lanes] = ksum[r, 5 * d + j, :, lanes] + totals[d]

    def depth(r, m):
        u = r * micro + m
        load = load_acts(r, m)
        load.start()
        load.wait()
        frame(r, m)
        widen(lambda g, par, lanes: framed[2 * g + par, :, lanes], 0, False, pairs + 2)

        @pl.loop(0, blocks)
        def _(b):
            made = conv(r, b, False)
            lanes = lane_block(b)
            for par in range(2):
                for q in range(pairs):
                    mixed[2 * q + par, :, lanes] = made[q, :, par * LANES : (par + 1) * LANES]

        store = pltpu.make_async_copy(mixed, saved.at[u], loads.at[3])
        store.start()
        store.wait()

    def weight_grad(r, m):
        u = r * micro + m
        load = pltpu.make_async_copy(saved.at[u], mixed, loads.at[3])
        load.start()
        load.wait()

        @pl.loop(0, rows // 8)
        def _(i):
            lines = pl.ds(i * 8, 8)
            wout[r] += lax.dot_general(
                mixed[lines].reshape(8 * cols, channels), gated[u, lines].reshape(8 * cols, channels),
                (((0,), (0,)), ((), ())), preferred_element_type=jnp.float32)

    runs = 2 * micro
    outer = jnp.logical_or(p == 0, p == sections - 1)
    early = jnp.where(outer, micro, 0)

    @pl.loop(0, 2 * runs)
    def _(i):
        is_depth = jnp.logical_and(i >= early, i < early + runs)
        k = jnp.where(i < early, i, jnp.where(is_depth, i - early, i - runs))
        r = lax.rem(first + k // micro, 2)
        m = lax.rem(k, micro)

        @pl.when(is_depth)
        def _():
            depth(r, m)

        @pl.when(jnp.logical_not(is_depth))
        def _():
            chain(r, m)

        ready = jnp.logical_or(
            jnp.logical_and(is_depth, k < early), jnp.logical_and(jnp.logical_not(is_depth), i >= early))

        @pl.when(ready)
        def _():
            weight_grad(r, m)

    for m in range(micro):
        drain(1 - first, m)
    for side in range(2):
        @pl.when(to_side[side])
        def _(side=side):
            act_copy(side).wait_send()
            for u in range(runs):
                halo_copy(u, side).wait_send()
    kout[...] = jnp.sum(ksum[...], axis=2)


def section_call(acts, masks, entry, weight, kern):
    _, _, _, micro, _, rows, cols, channels = acts.shape
    sections = lax.axis_size("sec")
    strips = lax.axis_size("strip")
    runs = 2 * micro
    blocks = channels // LANES
    dma = pltpu.SemaphoreType.DMA
    return pl.pallas_call(
        functools.partial(section_kernel, sections, strips, micro, rows, cols, channels),
        out_shape=(
            jax.ShapeDtypeStruct((2, micro, rows, cols, channels), BF),
            jax.ShapeDtypeStruct((2, channels, channels), jnp.float32),
            jax.ShapeDtypeStruct((2, 25, channels), jnp.float32),
            jax.ShapeDtypeStruct((runs, rows, cols, channels), BF),
        ),
        in_specs=[ANY, ANY, ANY, VMEM, VMEM],
        out_specs=(ANY, VMEM, VMEM, ANY),
        scratch_shapes=[
            pltpu.VMEM((runs, rows, cols, channels), BF),
            pltpu.VMEM((rows, cols, channels), jnp.int32),
            pltpu.VMEM((rows + 4, cols, channels), BF),
            pltpu.VMEM((2, 2, micro, 2, cols, channels), BF),
            pltpu.VMEM((rows, cols, channels), BF),
            pltpu.VMEM((runs, 2, 2, cols, channels), BF),
            pltpu.VMEM((runs, 2, 2, cols, channels), BF),
            pltpu.VMEM((blocks, 5, rows // 2 + 2, cols, PAIR), BF),
            pltpu.VMEM((micro, rows, cols, channels), BF),
            pltpu.VMEM((2, blocks, 15 * PAIR, PAIR), BF),
            pltpu.VMEM((2, 25, 8, channels), jnp.float32),
            dma((runs, blocks)),
            dma((runs, blocks)),
            dma((runs, 2)),
            dma((runs, 2)),
            dma((2,)),
            dma((2,)),
            dma((4,)),
            dma((runs,)),
        ],
        compiler_params=pltpu.CompilerParams(collective_id=0, has_side_effects=True, vmem_limit_bytes=63 << 20),
    )(acts, masks, entry, weight, kern)


def strip_sums(wide, taps):
    count = lax.axis_size("strip")
    place = lax.axis_index("strip")
    steps = count.bit_length() - 1
    share = wide.shape[0] // count
    columns = wide.shape[1]
    blocks = wide.reshape(count, share, columns)
    for step in range(steps):
        side = (place >> step) & 1
        pairs = blocks.reshape(-1, 2, share, columns)
        kept = lax.dynamic_index_in_dim(pairs, side, 1, keepdims=False)
        given = lax.dynamic_index_in_dim(pairs, 1 - side, 1, keepdims=False)
        sent = jnp.concatenate([given.reshape(-1, columns), taps]).astype(jnp.bfloat16)
        got = lax.ppermute(sent, "strip", [(i, i ^ (1 << step)) for i in range(count)]).astype(jnp.float32)
        rows = got.shape[0] - taps.shape[0]
        blocks = kept + got[:rows].reshape(kept.shape)
        taps = taps + got[rows:]
    return blocks.reshape(share, columns), taps


def body(activations, relu_masks, grad_in, mix_weight, depth_kernel):
    sections = lax.axis_size("sec")
    channels = activations.shape[-1]
    mirror = [(i, sections - 1 - i) for i in range(sections)]
    packed = jnp.concatenate([mix_weight[0, 0], depth_kernel[0, 0]], axis=0)
    mirrored = lax.ppermute(packed, "sec", mirror)
    weights = jnp.stack([mix_weight[0, 0], mirrored[:channels]])
    kernels = jnp.stack([depth_kernel[0, 0], mirrored[channels:]]).astype(jnp.float32)
    result, grads_w, grads_k, _ = section_call(activations, relu_masks, grad_in, weights, kernels)

    factor = 1.0 / H
    shares, kernel_all = strip_sums(
        jnp.concatenate([grads_w[0], grads_w[1]], axis=1), jnp.concatenate([grads_k[0], grads_k[1]], axis=1)
    )
    share_rows = shares.shape[0]
    partner = jnp.concatenate([shares[:, channels:], kernel_all[:, channels:]], axis=0).astype(BF)
    partner = lax.ppermute(partner, "sec", mirror).astype(jnp.float32)
    share_w = (shares[:, :channels] + partner[:share_rows]) * factor
    full_k = (kernel_all[:, :channels] + partner[share_rows:]) * factor
    return result[:, None, :, None], share_w[None, None], full_k[None, None]


def solution(mesh):
    placed = (
        P(None, "sec", None, None, None, "strip", None, None),
        P(None, "sec", None, None, None, "strip", None, None),
        P(None, None, None, "strip", None, None),
        P("sec", None, None, None),
        P("sec", None, None, None),
    )
    return jax.shard_map(
        body,
        mesh=mesh,
        in_specs=placed,
        out_specs=(
            P(None, "sec", None, None, "strip", None, None),
            P("sec", None, "strip", None),
            P("sec", None, None, None),
        ),
        check_vma=False,
    )
```

```python
import functools

import jax
import jax.numpy as jnp
from jax import lax
from jax.experimental import pallas as pl
from jax.experimental.pallas import tpu as pltpu
from jax.sharding import PartitionSpec as P

H = 256
LANES = 128
PAIR = 2 * LANES
BF = jnp.bfloat16
ANY = pl.BlockSpec(memory_space=pl.ANY)
VMEM = pl.BlockSpec(memory_space=pltpu.VMEM)
MESH = pl.DeviceIdType.MESH


def lane_block(block):
    return pl.ds(pl.multiple_of(block * LANES, LANES), LANES)


def shifted(value, offset, column):
    if offset == 0:
        return value
    cols = value.shape[0]
    turned = pltpu.roll(value, (-offset) % cols, 0)
    inside = column < cols - offset if offset > 0 else column >= -offset
    return jnp.where(inside, turned, 0.0)


def spread_kernel(kern, conv_w):
    blocks = conv_w.shape[0]
    same = lax.broadcasted_iota(jnp.int32, (LANES, LANES), 0) == lax.broadcasted_iota(jnp.int32, (LANES, LANES), 1)

    @pl.loop(0, blocks)
    def _(b):
        lanes = lane_block(b)
        for j in range(5):
            for t in range(3):
                for e in range(2):
                    for f in range(2):
                        d = 2 * t + e - f
                        if 0 <= d < 5:
                            tap = jnp.broadcast_to(kern[pl.ds(5 * d + j, 1), lanes], (LANES, LANES))
                            tile = jnp.where(same, tap, 0.0).astype(BF)
                        else:
                            tile = jnp.zeros((LANES, LANES), BF)
                        conv_w[b, pl.ds((3 * j + t) * PAIR + e * LANES, LANES), f * LANES : (f + 1) * LANES] = tile


def section_kernel(
    sections, strips, micro, rows, cols, channels,
    acts, masks, entry, weight, kern, mask_out,
    sg, wout, kout, saved, mask_in,
    gated, seen, framed, act_halo, mixed, edge, halo, wide, out, conv_w, ksum,
    send, recv, halo_send, halo_recv, act_send, act_recv, loads, stores, entries, deep, near_w, near_k, skip_send, near_send, near_recv,
):
    p = lax.axis_index("sec")
    s = lax.axis_index("strip")
    blocks = channels // LANES
    pairs = rows // 2
    first = 1 - (2 * p) // sections
    short = sections == 4
    outer = jnp.logical_or(p == 0, p == sections - 1)
    column = lax.broadcasted_iota(jnp.int32, (cols, LANES), 0)

    barrier = pltpu.get_barrier_semaphore()
    near = [(p > 0, (p - 1, s)), (p < sections - 1, (p + 1, s)), (s > 0, (p, s - 1)), (s < strips - 1, (p, s + 1))]
    if short:
        near += [(p < 2, (p + 2, s)), (p >= 2, (p - 2, s))]
    for there, device in near:
        @pl.when(there)
        def _(device=device):
            pl.semaphore_signal(barrier, inc=1, device_id=device, device_id_type=MESH)
    pl.semaphore_wait(barrier, sum(jnp.where(there, 1, 0) for there, _ in near))

    to_side = [s < strips - 1, s > 0]
    from_side = [s > 0, s < strips - 1]
    side_of = [(p, s + 1), (p, s - 1)]

    def act_copy(side):
        lines = pl.ds(rows - 2, 2) if side == 0 else pl.ds(0, 2)
        return pltpu.make_async_remote_copy(
            src_ref=acts.at[:, 0, 0, :, 0, lines], dst_ref=act_halo.at[side],
            send_sem=act_send.at[side], recv_sem=act_recv.at[side], device_id=side_of[side], device_id_type=MESH)

    def halo_copy(u, side):
        return pltpu.make_async_remote_copy(
            src_ref=edge.at[u, side], dst_ref=halo.at[u, side],
            send_sem=halo_send.at[u, side], recv_sem=halo_recv.at[u, side], device_id=side_of[side], device_id_type=MESH)

    def main_copy(r, m, b):
        u = r * micro + m
        lanes = lane_block(b)
        return pltpu.make_async_remote_copy(
            src_ref=out.at[m, :, :, lanes], dst_ref=gated.at[u, :, :, lanes],
            send_sem=send.at[u, b], recv_sem=recv.at[u, b], device_id=(p + 2 * r - 1, s), device_id_type=MESH)

    def skip_copy(r, m, b):
        u = r * micro + m
        lanes = lane_block(b)
        return pltpu.make_async_remote_copy(
            src_ref=out.at[m, :, :, lanes], dst_ref=gated.at[u, :, :, lanes],
            send_sem=skip_send.at[m, b], recv_sem=recv.at[u, b], device_id=(p + 4 * r - 2, s), device_id_type=MESH)

    def near_copies():
        device = 3 * (p // 2)
        pieces = [(weight.at[1 - first], near_w), (kern.at[1 - first], near_k)]
        pieces += [(mask_out.at[m], mask_in.at[m]) for m in range(micro)]
        return [
            pltpu.make_async_remote_copy(
                src_ref=src, dst_ref=dst, send_sem=near_send.at[n], recv_sem=near_recv.at[n],
                device_id=(device, s), device_id_type=MESH)
            for n, (src, dst) in enumerate(pieces)
        ]

    def sends(r):
        if short:
            return jnp.logical_and(has_next(r), p != 1 + r)
        return has_next(r)

    def skips(r):
        return p == 2 - r

    def start_sends(r, m, b):
        @pl.when(sends(r))
        def _():
            main_copy(r, m, b).start()

        if short:
            @pl.when(skips(r))
            def _():
                skip_copy(r, m, b).start()

    def has_next(r):
        return jnp.logical_or(jnp.logical_and(r == 0, p > 0), jnp.logical_and(r == 1, p < sections - 1))

    def out_store(r, m):
        return pltpu.make_async_copy(out.at[m], sg.at[r, m], stores.at[r * micro + m])

    def drain(r, m):
        @pl.when(sends(r))
        def _():
            @pl.loop(0, blocks)
            def _(b):
                main_copy(r, m, b).wait_send()

        if short:
            @pl.when(skips(r))
            def _():
                @pl.loop(0, blocks)
                def _(b):
                    skip_copy(r, m, b).wait_send()

        out_store(r, m).wait()

    if short:
        @pl.when(jnp.logical_not(outer))
        def _():
            for copy in near_copies():
                copy.start()

    for side in range(2):
        @pl.when(to_side[side])
        def _(side=side):
            act_copy(side).start()

        @pl.when(jnp.logical_not(from_side[side]))
        def _(side=side):
            act_halo[side] = jnp.zeros_like(act_halo[side])

    spread_kernel(kern.at[first], conv_w.at[first])
    ksum[...] = jnp.zeros_like(ksum)
    wout[...] = jnp.zeros_like(wout)
    for side in range(2):
        @pl.when(from_side[side])
        def _(side=side):
            act_copy(side).wait_recv()

    def widen(line_of, place, swap, count):
        @pl.loop(0, count * blocks)
        def _(i):
            g = i // blocks
            b = i % blocks
            for par in range(2):
                value = line_of(g, par, lane_block(b)).astype(jnp.float32)
                at = (1 - par if swap else par) * LANES
                for j in range(5):
                    wide[b, j, place + g, :, at : at + LANES] = shifted(value, j - 2, column).astype(BF)

    runs = 2 * micro
    early = jnp.where(outer, micro, 0)

    def place_of(i):
        is_depth = jnp.logical_and(i >= early, i < early + runs)
        k = jnp.where(i < early, i, jnp.where(is_depth, i - early, i - runs))
        return is_depth, k, lax.rem(first + k // micro, 2), lax.rem(k, micro)

    def load_entry(r, m):
        return pltpu.make_async_copy(entry.at[r, m, 0], gated.at[r * micro + m], entries.at[m])

    def load_depth(u):
        return pltpu.make_async_copy(saved.at[u], deep, loads.at[3])

    def store_depth(u):
        return pltpu.make_async_copy(deep, saved.at[u], loads.at[2])

    def fetch_next(i):
        @pl.when(i + 1 < 2 * runs)
        def _():
            _, _, r, m = place_of(i + 1)
            load_acts(r, m).start()

    def load_acts(r, m):
        return pltpu.make_async_copy(acts.at[r, 0, 0, m, 0], framed.at[pl.ds(2, rows)], loads.at[0])

    def frame(r, m):
        framed[pl.ds(0, 2)] = act_halo[0, r, m]
        framed[pl.ds(rows + 2, 2)] = act_halo[1, r, m]

    def conv(r, b, flip):
        parts = []
        for j in range(5):
            for t in range(3):
                part = wide[b, 4 - j, pl.ds(2 - t, pairs)] if flip else wide[b, j, pl.ds(t, pairs)]
                parts.append(part.reshape(pairs * cols, PAIR))
        made = jnp.dot(jnp.concatenate(parts, axis=1), conv_w[r, b], preferred_element_type=jnp.float32)
        return made.astype(BF).reshape(pairs, cols, PAIR)

    def mix(u, h, mixer):
        ends = jnp.concatenate([gated[u, pl.ds(rows - 2, 2)], gated[u, pl.ds(0, 2)]], axis=0)
        made = lax.dot_general(ends.reshape(4 * cols, channels), mixer[...], (((1,), (1,)), ((), ())),
                               preferred_element_type=jnp.float32)
        edge[h] = made.astype(BF).reshape(2, 2, cols, channels)
        for side in range(2):
            @pl.when(to_side[side])
            def _(side=side):
                halo_copy(h, side).start()

            @pl.when(jnp.logical_not(from_side[side]))
            def _(side=side):
                halo[h, side] = jnp.zeros_like(halo[h, side])

        @pl.loop(0, rows // 16)
        def _(i):
            lines = pl.ds(i * 16, 16)
            got = lax.dot_general(gated[u, lines].reshape(16 * cols, channels), mixer[...], (((1,), (1,)), ((), ())),
                                  preferred_element_type=jnp.float32)
            mixed[lines] = got.astype(BF).reshape(16, cols, channels)

        widen(lambda g, par, lanes: mixed[2 * g + par, :, lanes], 1, True, pairs)
        for side in range(2):
            @pl.when(from_side[side])
            def _(side=side):
                halo_copy(h, side).wait_recv()
        widen(lambda g, par, lanes: halo[h, 0, par, :, lanes], 0, True, 1)
        widen(lambda g, par, lanes: halo[h, 1, par, :, lanes], pairs + 1, True, 1)

    def step_ahead(r, m):
        u = r * micro + m
        copies = near_copies()

        @pl.when(m == 0)
        def _():
            copies[0].wait_recv()
            copies[1].wait_recv()
            spread_kernel(near_k, conv_w.at[first])

        for n in range(micro):
            @pl.when(m == n)
            def _(n=n):
                copies[2 + n].wait_recv()

        load = pltpu.make_async_copy(mask_in.at[m], deep, loads.at[3])
        load.start()
        load.wait()

        @pl.loop(0, rows)
        def _(row):
            value = gated[u, row].astype(jnp.float32)
            gated[u, row] = jnp.where(deep[row].astype(jnp.float32) == 1.0, value, 0.0).astype(BF)

        mix(u, runs + m, near_w)

        @pl.loop(0, blocks)
        def _(b):
            made = conv(first, b, True)
            lanes = lane_block(b)
            for par in range(2):
                for q in range(pairs):
                    gated[u, 2 * q + par, :, lanes] = made[q, :, (1 - par) * LANES : (2 - par) * LANES]

    def correlate(r, b):
        lanes = lane_block(b)
        group = 4
        for j in range(5):
            totals = [jnp.zeros((8, LANES), jnp.float32)] * 5
            for q in range(0, rows, group):
                near_rows = [framed[q + k, :, lanes].reshape(cols // 16, 16, LANES) for k in range(group + 4)]
                lines = []
                for h in range(group):
                    at = (1 - h % 2) * LANES
                    lines.append(wide[b, 4 - j, (q + h) // 2 + 1, :, at : at + LANES].reshape(cols // 16, 16, LANES))
                for d in range(5):
                    terms = []
                    for h in range(group):
                        part = lines[h] * near_rows[h + d]
                        terms += [part[k] for k in range(cols // 16)]
                    while len(terms) > 1:
                        terms = [terms[k] + terms[k + 1] for k in range(0, len(terms), 2)]
                    short = jnp.sum(terms[0].astype(jnp.float32).reshape(2, 8, LANES), axis=0)
                    totals[d] = totals[d] + short
            for d in range(5):
                ksum[r, 5 * d + j, :, lanes] = ksum[r, 5 * d + j, :, lanes] + totals[d]

    def chain(i, r, m):
        u = r * micro + m
        load_mask = pltpu.make_async_copy(masks.at[r, 0, 0, m, 0], seen, loads.at[1])
        load_mask.start()
        fresh = jnp.logical_not(has_next(1 - r))

        @pl.when(fresh)
        def _():
            load_entry(r, m).wait()

        @pl.when(jnp.logical_not(fresh))
        def _():
            @pl.loop(0, blocks)
            def _(b):
                main_copy(r, m, b).wait_recv()

        if short:
            @pl.when(jnp.logical_and(outer, r != first))
            def _():
                step_ahead(r, m)

        @pl.when(i >= early)
        def _():
            load_depth(u).start()

        load_mask.wait()

        @pl.loop(0, rows)
        def _(row):
            value = gated[u, row].astype(jnp.float32)
            gated[u, row] = jnp.where(seen[row] == 1, value, 0.0).astype(BF)

        mix(u, u, weight.at[r])
        load_acts(r, m).wait()
        frame(r, m)

        @pl.when(r != first)
        def _():
            drain(first, m)

        @pl.loop(0, blocks)
        def _(b):
            made = conv(r, b, True)
            correlate(r, b)
            lanes = lane_block(b)
            for par in range(2):
                piece = made[:, :, (1 - par) * LANES : (2 - par) * LANES]
                for q in range(pairs):
                    out[m, 2 * q + par, :, lanes] = piece[q]

            start_sends(r, m, b)

        out_store(r, m).start()
        fetch_next(i)

    def depth(i, k, r, m):
        u = r * micro + m
        load_acts(r, m).wait()
        frame(r, m)

        @pl.when(k == micro)
        def _():
            spread_kernel(kern.at[r], conv_w.at[r])

        widen(lambda g, par, lanes: framed[2 * g + par, :, lanes], 0, False, pairs + 2)
        fetch_next(i)

        @pl.when(k > 0)
        def _():
            store_depth(u).wait()

        @pl.loop(0, blocks)
        def _(b):
            made = conv(r, b, False)
            lanes = lane_block(b)
            for par in range(2):
                for q in range(pairs):
                    deep[2 * q + par, :, lanes] = made[q, :, par * LANES : (par + 1) * LANES]

        store_depth(u).start()

        @pl.when(k == runs - 1)
        def _():
            store_depth(u).wait()

    def weight_grad(late, r, m):
        u = r * micro + m

        @pl.when(late)
        def _():
            load_depth(u).wait()

        @pl.loop(0, rows // 8)
        def _(i):
            lines = pl.ds(i * 8, 8)
            wout[r] += lax.dot_general(
                deep[lines].reshape(8 * cols, channels), gated[u, lines].reshape(8 * cols, channels),
                (((0,), (0,)), ((), ())), preferred_element_type=jnp.float32)

    load_acts(*place_of(0)[2:]).start()

    @pl.when(outer)
    def _():
        for m in range(micro):
            load_entry(first, m).start()

    @pl.loop(0, 2 * runs)
    def _(i):
        is_depth, k, r, m = place_of(i)

        @pl.when(is_depth)
        def _():
            depth(i, k, r, m)

        @pl.when(jnp.logical_not(is_depth))
        def _():
            chain(i, r, m)

        late = jnp.logical_and(jnp.logical_not(is_depth), i >= early)
        ready = jnp.logical_or(jnp.logical_and(is_depth, k < early), late)

        @pl.when(ready)
        def _():
            weight_grad(late, r, m)

    for m in range(micro):
        drain(1 - first, m)
    for side in range(2):
        @pl.when(to_side[side])
        def _(side=side):
            act_copy(side).wait_send()
            for u in range(runs):
                halo_copy(u, side).wait_send()

            if short:
                @pl.when(outer)
                def _():
                    for m in range(micro):
                        halo_copy(runs + m, side).wait_send()

    if short:
        @pl.when(jnp.logical_not(outer))
        def _():
            for copy in near_copies():
                copy.wait_send()
    kout[...] = jnp.sum(ksum[...], axis=2)


def section_call(acts, masks, entry, weight, kern, mask_out):
    _, _, _, micro, _, rows, cols, channels = acts.shape
    sections = lax.axis_size("sec")
    strips = lax.axis_size("strip")
    runs = 2 * micro
    blocks = channels // LANES
    dma = pltpu.SemaphoreType.DMA
    return pl.pallas_call(
        functools.partial(section_kernel, sections, strips, micro, rows, cols, channels),
        out_shape=(
            jax.ShapeDtypeStruct((2, micro, rows, cols, channels), BF),
            jax.ShapeDtypeStruct((2, channels, channels), jnp.float32),
            jax.ShapeDtypeStruct((2, 25, channels), jnp.float32),
            jax.ShapeDtypeStruct((runs, rows, cols, channels), BF),
            jax.ShapeDtypeStruct((micro, rows, cols, channels), BF),
        ),
        in_specs=[ANY, ANY, ANY, VMEM, VMEM, ANY],
        out_specs=(ANY, VMEM, VMEM, ANY, ANY),
        scratch_shapes=[
            pltpu.VMEM((runs, rows, cols, channels), BF),
            pltpu.VMEM((rows, cols, channels), jnp.int32),
            pltpu.VMEM((rows + 4, cols, channels), BF),
            pltpu.VMEM((2, 2, micro, 2, cols, channels), BF),
            pltpu.VMEM((rows, cols, channels), BF),
            pltpu.VMEM((runs + micro, 2, 2, cols, channels), BF),
            pltpu.VMEM((runs + micro, 2, 2, cols, channels), BF),
            pltpu.VMEM((blocks, 5, rows // 2 + 2, cols, PAIR), BF),
            pltpu.VMEM((micro, rows, cols, channels), BF),
            pltpu.VMEM((2, blocks, 15 * PAIR, PAIR), BF),
            pltpu.VMEM((2, 25, 8, channels), jnp.float32),
            dma((runs, blocks)),
            dma((runs, blocks)),
            dma((runs + micro, 2)),
            dma((runs + micro, 2)),
            dma((2,)),
            dma((2,)),
            dma((4,)),
            dma((runs,)),
            dma((micro,)),
            pltpu.VMEM((rows, cols, channels), BF),
            pltpu.VMEM((channels, channels), BF),
            pltpu.VMEM((25, channels), jnp.float32),
            dma((micro, blocks)),
            dma((2 + micro,)),
            dma((2 + micro,)),
        ],
        compiler_params=pltpu.CompilerParams(collective_id=0, has_side_effects=True, vmem_limit_bytes=63 << 20),
    )(acts, masks, entry, weight, kern, mask_out)


def strip_sums(wide, taps):
    count = lax.axis_size("strip")
    place = lax.axis_index("strip")
    steps = count.bit_length() - 1
    share = wide.shape[0] // count
    columns = wide.shape[1]
    blocks = wide.reshape(count, share, columns)
    for step in range(steps):
        side = (place >> step) & 1
        pairs = blocks.reshape(-1, 2, share, columns)
        kept = lax.dynamic_index_in_dim(pairs, side, 1, keepdims=False)
        given = lax.dynamic_index_in_dim(pairs, 1 - side, 1, keepdims=False)
        sent = jnp.concatenate([given.reshape(-1, columns), taps]).astype(jnp.bfloat16)
        got = lax.ppermute(sent, "strip", [(i, i ^ (1 << step)) for i in range(count)]).astype(jnp.float32)
        rows = got.shape[0] - taps.shape[0]
        blocks = kept + got[:rows].reshape(kept.shape)
        taps = taps + got[rows:]
    return blocks.reshape(share, columns), taps


def body(activations, relu_masks, grad_in, mix_weight, depth_kernel):
    sections = lax.axis_size("sec")
    channels = activations.shape[-1]
    mirror = [(i, sections - 1 - i) for i in range(sections)]
    packed = jnp.concatenate([mix_weight[0, 0], depth_kernel[0, 0]], axis=0)
    mirrored = lax.ppermute(packed, "sec", mirror)
    weights = jnp.stack([mix_weight[0, 0], mirrored[:channels]])
    kernels = jnp.stack([depth_kernel[0, 0], mirrored[channels:]]).astype(jnp.float32)
    inner = (2 * lax.axis_index("sec")) // sections
    mask_out = lax.dynamic_index_in_dim(relu_masks[:, 0, 0, :, 0], inner, 0, keepdims=False)
    mask_out = (mask_out == 1).astype(BF)
    result, grads_w, grads_k, _, _ = section_call(activations, relu_masks, grad_in, weights, kernels, mask_out)

    factor = 1.0 / H
    shares, kernel_all = strip_sums(
        jnp.concatenate([grads_w[0], grads_w[1]], axis=1), jnp.concatenate([grads_k[0], grads_k[1]], axis=1)
    )
    share_rows = shares.shape[0]
    partner = jnp.concatenate([shares[:, channels:], kernel_all[:, channels:]], axis=0).astype(BF)
    partner = lax.ppermute(partner, "sec", mirror).astype(jnp.float32)
    share_w = (shares[:, :channels] + partner[:share_rows]) * factor
    full_k = (kernel_all[:, :channels] + partner[share_rows:]) * factor
    return result[:, None, :, None], share_w[None, None], full_k[None, None]


def solution(mesh):
    placed = (
        P(None, "sec", None, None, None, "strip", None, None),
        P(None, "sec", None, None, None, "strip", None, None),
        P(None, None, None, "strip", None, None),
        P("sec", None, None, None),
        P("sec", None, None, None),
    )
    return jax.shard_map(
        body,
        mesh=mesh,
        in_specs=placed,
        out_specs=(
            P(None, "sec", None, None, "strip", None, None),
            P("sec", None, "strip", None),
            P("sec", None, None, None),
        ),
        check_vma=False,
    )
```
